32 devices in a mesh: row: 8 (over y, x, core), col: 4 (over z).
Axes of the slice: x: 2, y: 2, z: 4, core: 2. Of those that a mesh axis runs over, the one named last changes fastest.
Arguments:
- diag_block: float32 [512, 512], P('row', 'col'), may hold values from 0 to 2.5, as said below
- panel_below: float32 [24576, 512], P('row', 'col'), may hold values from -1.8 to 1.8
- trailing: float32 [24576, 6144], P('row', 'col'), may hold values from -6 to 6
Outputs:
- diag_factor: float32 [512, 512], P('row', 'col')
- panel_factor: float32 [24576, 512], P('row', 'col')
- new_trailing: float32 [24576, 6144], P('row', 'col')
The draws below stay inside these ranges and needn't reach their ends.
Inputs may be any that keep to these rules, and one draw needn't show every extreme that they name: `diag_block`: taken to matrix order in both dimensions, the block is symmetric with all eigenvalues 0.5 or more.
All inputs are finite; a program needn't handle non-finite values.
Results may differ from the reference program's by a relative error of at most 0.00015.
Values sent between devices are 32-bit elements; how exact they have to be, the bound alone decides.
A program may use at most 128 MiB of HBM per device.

```python
import jax
import jax.numpy as jnp
from jax import lax

NB = 512
TC = 6144
BELOW = 24576
N_ROW = 8
N_COL = 4


def draw_diag_block(key, part):
    key_points, key_ridge = jax.random.split(key)
    points = jax.random.uniform(key_points, (NB, 3), jnp.float32, 0.0, 1.0)
    ridge = jax.random.uniform(key_ridge, (NB,), jnp.float32, 0.5, 1.5)
    index = jnp.arange(NB, dtype=jnp.int32)
    rows_block = NB // N_ROW
    cols_block = NB // N_COL
    row_map = index % rows_block * N_ROW + index // rows_block
    col_map = index % cols_block * N_COL + index // cols_block
    row_points = points[row_map]
    col_points = points[col_map]
    distance = jnp.zeros((NB, NB), jnp.float32)
    for coord in range(3):
        gap = row_points[:, coord][:, None] - col_points[:, coord][None, :]
        distance = distance + gap * gap
    length_scale = 0.6 / NB ** (1.0 / 3.0)
    kernel = jnp.exp(-distance / (2.0 * length_scale * length_scale))
    same = row_map[:, None] == col_map[None, :]
    kernel = kernel + jnp.where(same, ridge[row_map][:, None], 0.0)
    return kernel.astype(jnp.float32)


def level_of(key, dims, pieces, least, top_value):
    level = 1.0
    for position, blocks in pieces:
        heights = jax.random.uniform(jax.random.fold_in(jax.random.fold_in(key, 6), position), (blocks,), jnp.float32, least / len(pieces), top_value / len(pieces))
        level = level * jnp.repeat(jnp.exp(heights), dims[position] // blocks).reshape((-1,) + (1,) * (len(dims) - 1 - position))
    return level


def gaussian(stream_key, dims, width, reach, cuts=(), kind=jnp.bfloat16):
    level = level_of(stream_key, dims, cuts, -0.22, 0.18) if cuts else 1.0
    values = jax.random.normal(stream_key, dims, jnp.float32) * width * level
    return jnp.minimum(jnp.maximum(values, -reach), reach).astype(kind)


def setup_inputs(seed: int = 0) -> dict:
    arg_keys = jax.random.split(jax.random.key(seed), 4)
    diag_block = draw_diag_block(jax.random.fold_in(arg_keys[3], 71), 0)
    panel_below = gaussian(arg_keys[1], (BELOW, NB), 0.3, 1.8, ((0, 8), (1, 4)), jnp.float32)
    trailing = gaussian(arg_keys[2], (BELOW, TC), 1.0, 6.0, ((0, 8), (1, 4)), jnp.float32)
    return {"diag_block": diag_block, "panel_below": panel_below, "trailing": trailing}


def to_matrix(array, parts, axis):
    moved = jnp.moveaxis(array, axis, 0)
    length = moved.shape[0]
    shaped = moved.reshape((parts, length // parts) + moved.shape[1:])
    shaped = jnp.swapaxes(shaped, 0, 1).reshape(moved.shape)
    return jnp.moveaxis(shaped, 0, axis)

def to_storage(array, parts, axis):
    moved = jnp.moveaxis(array, axis, 0)
    length = moved.shape[0]
    shaped = moved.reshape((length // parts, parts) + moved.shape[1:])
    shaped = jnp.swapaxes(shaped, 0, 1).reshape(moved.shape)
    return jnp.moveaxis(shaped, 0, axis)

def reference(diag_block, panel_below, trailing):
    diag_matrix = to_matrix(to_matrix(diag_block, N_ROW, 0), N_COL, 1)
    factor = jnp.linalg.cholesky(diag_matrix)
    diag_factor = to_storage(to_storage(factor, N_ROW, 0), N_COL, 1)
    identity = jnp.eye(NB, dtype=jnp.float32)
    inverse = lax.linalg.triangular_solve(factor, identity, left_side=True, lower=True)
    panel_matrix = to_matrix(panel_below, N_COL, 1)
    solved = jnp.dot(panel_matrix.astype(jnp.float32), inverse.T.astype(jnp.float32), precision=lax.Precision.HIGHEST, preferred_element_type=jnp.float32)
    panel_factor = to_storage(solved, N_COL, 1)
    solved_matrix = to_matrix(solved, N_ROW, 0)
    top_store = to_storage(solved_matrix[:TC], N_COL, 0)
    update = jnp.dot(solved.astype(jnp.float32), top_store.T.astype(jnp.float32), precision=lax.Precision.HIGHEST, preferred_element_type=jnp.float32)
    new_trailing = trailing - update
    return (diag_factor, panel_factor, new_trailing)
```

```python
import functools

import jax
import jax.numpy as jnp
from jax import lax
from jax.experimental import pallas as pl
from jax.experimental.pallas import tpu as pltpu
from jax.sharding import PartitionSpec as P

BLOCK = 128
TILE = 8


def full_dot(left, right, dims):
    return lax.dot_general(
        left, right, (dims, ((), ())), precision=lax.Precision.HIGHEST, preferred_element_type=jnp.float32
    )


def eliminate(s_ref, r_ref, base):
    count = BLOCK // TILE
    shape = (TILE, BLOCK)
    lane = lax.broadcasted_iota(jnp.int32, shape, 1)
    tiles = [s_ref[base + t * TILE : base + (t + 1) * TILE, base : base + BLOCK] for t in range(count)]
    for p in range(count):
        first = p * TILE
        own = tiles[p]
        rows = [jnp.broadcast_to(own[j : j + 1, :], shape) for j in range(TILE)]
        a = [
            [jnp.broadcast_to(rows[i][:, first + j : first + j + 1], shape) for j in range(i + 1)]
            for i in range(TILE)
        ]
        cols = {
            t: [jnp.broadcast_to(tiles[t][:, first + j : first + j + 1], shape) for j in range(TILE)]
            for t in range(p + 1, count)
        }
        for k in range(TILE):
            scale = lax.rsqrt(a[k][k])
            low = [a[i][k] * scale for i in range(k + 1, TILE)]
            row = rows[k] * scale
            r_ref[first + k : first + k + 1, :] = row[0:1, :]
            used = row + jnp.where(lane == first + k, scale, 0.0)
            for i in range(k + 1, TILE):
                rows[i] = rows[i] - low[i - k - 1] * used
                for j in range(k + 1, i + 1):
                    a[i][j] = a[i][j] - low[i - k - 1] * low[j - k - 1]
            for t in range(p + 1, count):
                col = cols[t][k] * scale
                tiles[t] = tiles[t] - col * used
                for j in range(k + 1, TILE):
                    cols[t][j] = cols[t][j] - col * low[j - k - 1]


def split(value):
    high = value.astype(jnp.bfloat16)
    return high, (value - high.astype(jnp.float32)).astype(jnp.bfloat16)


def split_rows(value):
    high, low = split(value)
    return jnp.concatenate([high, high, low], axis=0)


def split_dot(left, right_parts):
    high, low = split(left)
    return lax.dot_general(
        jnp.concatenate([high, low, high], axis=1),
        right_parts,
        (((1,), (0,)), ((), ())),
        preferred_element_type=jnp.float32,
    )


def chol_kernel(row_count, col_count, a_ref, f_ref, q_ref, s_ref, l_ref, x_ref, r_ref):
    width = a_ref.shape[0]
    s_ref[...] = a_ref[...]
    l_ref[...] = jnp.zeros_like(l_ref)
    x_ref[...] = jnp.zeros_like(x_ref)
    up = lax.broadcasted_iota(jnp.int32, (BLOCK, BLOCK), 0)
    across = lax.broadcasted_iota(jnp.int32, (BLOCK, BLOCK), 1)
    for base in range(0, width, BLOCK):
        end = base + BLOCK
        eliminate(s_ref, r_ref, base)
        both = r_ref[...]
        l_ref[base:end, base:end] = jnp.where(up >= across, both.T, 0.0)
        inv = jnp.where(up > across, both, 0.0) + jnp.where(up == across, 1.0 / both, 0.0)
        x_ref[base:end, base:end] = inv
        if base:
            x_ref[base:end, :base] = -full_dot(
                inv, full_dot(l_ref[base:end, :base], x_ref[:base, :base], ((1,), (0,))), ((1,), (0,))
            )
        if end < width:
            below = full_dot(s_ref[end:, base:end], inv, ((1,), (1,)))
            l_ref[end:, base:end] = below
            s_ref[end:, end:] = s_ref[end:, end:] - full_dot(below, below, ((1,), (1,)))
    per = width // col_count
    store = lax.broadcasted_iota(jnp.int32, (width, width), 0)
    natural = lax.broadcasted_iota(jnp.int32, (width, width), 1)
    move = jnp.where(natural == (store % per) * col_count + store // per, 1.0, 0.0)
    s_ref[...] = full_dot(full_dot(move, x_ref[...], ((1,), (0,))), move, ((1,), (1,)))
    q_ref[...] = split_rows(s_ref[...].T)
    rows_dev = width // row_count
    r = lax.axis_index("row")
    c = lax.axis_index("col")
    i0 = lax.broadcasted_iota(jnp.int32, (rows_dev, width), 0)
    i1 = lax.broadcasted_iota(jnp.int32, (rows_dev, width), 1)
    pick_rows = jnp.where(i1 == i0 * row_count + r, 1.0, 0.0)
    j0 = lax.broadcasted_iota(jnp.int32, (per, width), 0)
    j1 = lax.broadcasted_iota(jnp.int32, (per, width), 1)
    pick_cols = jnp.where(j1 == j0 * col_count + c, 1.0, 0.0)
    f_ref[...] = full_dot(full_dot(pick_rows, l_ref[...], ((1,), (0,))), pick_cols, ((1,), (1,)))


def factorize(diag_matrix, row_count, col_count):
    width = diag_matrix.shape[0]
    tripled = jax.ShapeDtypeStruct((3 * width, width), jnp.bfloat16)
    return pl.pallas_call(
        functools.partial(chol_kernel, row_count, col_count),
        out_shape=(jax.ShapeDtypeStruct((width // row_count, width // col_count), jnp.float32), tripled),
        scratch_shapes=[pltpu.VMEM((width, width), jnp.float32)] * 3 + [pltpu.VMEM((BLOCK, BLOCK), jnp.float32)],
        compiler_params=pltpu.CompilerParams(vmem_limit_bytes=32 * 1024 * 1024),
    )(diag_matrix)


def top_kernel(col_count, g_ref, q_ref, o_ref, t_ref):
    groups, length, lanes = g_ref.shape
    owners = groups // col_count
    width = q_ref.shape[1]
    for h in range(owners):
        left = jnp.concatenate([g_ref[h * col_count + z] for z in range(col_count)], axis=1)
        solved = split_dot(left, q_ref[...])
        for b in range(width // BLOCK):
            t_ref[b, pl.ds(h, length, stride=owners), :] = solved[:, b * BLOCK : (b + 1) * BLOCK]
    for b in range(width // BLOCK):
        high, low = split(t_ref[b].T)
        at = b * BLOCK
        o_ref[at : at + BLOCK, :] = high
        o_ref[width + at : width + at + BLOCK, :] = high
        o_ref[2 * width + at : 2 * width + at + BLOCK, :] = low


def solve_top(gathered, q_parts, col_count):
    groups, length, lanes = gathered.shape
    width = q_parts.shape[1]
    columns = groups // col_count * length
    return pl.pallas_call(
        functools.partial(top_kernel, col_count),
        out_shape=jax.ShapeDtypeStruct((3 * width, columns), jnp.bfloat16),
        scratch_shapes=[pltpu.VMEM((width // BLOCK, columns, BLOCK), jnp.float32)],
        compiler_params=pltpu.CompilerParams(vmem_limit_bytes=56 * 1024 * 1024),
    )(gathered, q_parts)


def update_kernel(col_count, p_ref, q_ref, t_ref, c_ref, *refs):
    f_ref, n_ref, s_ref = refs[-3:]
    left = jnp.concatenate([p_ref[z] for z in range(col_count)], axis=1)
    solved = split_dot(left, q_ref[...])
    lanes = f_ref.shape[1]
    for z in range(col_count):
        s_ref[z] = solved[:, z * lanes : (z + 1) * lanes]
    f_ref[...] = s_ref[lax.axis_index("col")]
    n_ref[...] = c_ref[...] - split_dot(solved, t_ref[...])


def update_rows(panel, q_parts, top_parts, trailing, offset, previous, col_count):
    _, length, lanes = panel.shape
    rows, columns = trailing.shape
    tile = 256
    first = offset // tile
    fixed = lambda a: pl.BlockSpec(a.shape, lambda i: (0, 0), pipeline_mode=pl.Buffered(1))
    strip = lambda n: pl.BlockSpec((tile, n), lambda i: (first + i, 0))
    flops = 2 * 3 * length * q_parts.shape[1] * (columns + q_parts.shape[1])
    return pl.pallas_call(
        functools.partial(update_kernel, col_count),
        grid=(length // tile,),
        out_shape=(
            jax.ShapeDtypeStruct((rows, lanes), jnp.float32),
            jax.ShapeDtypeStruct((rows, columns), jnp.float32),
        ),
        in_specs=[
            pl.BlockSpec((col_count, tile, lanes), lambda i: (0, i, 0)),
            fixed(q_parts),
            fixed(top_parts),
            strip(columns),
        ]
        + [pl.BlockSpec(memory_space=pl.ANY)] * len(previous),
        out_specs=(strip(lanes), strip(columns)),
        scratch_shapes=[pltpu.VMEM((col_count, tile, lanes), jnp.float32)],
        input_output_aliases={4 + i: i for i in range(len(previous))},
        cost_estimate=pl.CostEstimate(
            flops=flops, bytes_accessed=length * columns * 8, transcendentals=0
        ),
        compiler_params=pltpu.CompilerParams(vmem_limit_bytes=40 * 1024 * 1024),
    )(panel, q_parts, top_parts, trailing, *previous)


CHUNKS = 4


def to_matrix(gathered, row_count, col_count):
    _, _, m, n = gathered.shape
    return gathered.transpose(2, 0, 3, 1).reshape(m * row_count, n * col_count)


def shards(diag_block, panel_below, trailing):
    row_count = lax.axis_size("row")
    col_count = lax.axis_size("col")
    owners = row_count // col_count
    top_length = trailing.shape[1] // owners
    pairs = [
        ((h * col_count + c) * col_count + z, (h * col_count + z) * col_count + c)
        for h in range(owners)
        for c in range(col_count)
        for z in range(col_count)
    ]
    diag = lax.all_gather(lax.all_gather(diag_block, "col"), "row")
    diag_matrix = to_matrix(diag, row_count, col_count)
    mine = lax.ppermute(panel_below[:top_length], ("row", "col"), pairs)
    mine, _ = lax.optimization_barrier((mine, diag))
    tops = lax.all_gather(mine, "row")
    length = panel_below.shape[0] // CHUNKS
    panels = []
    last = tops
    for i in range(CHUNKS):
        piece = panel_below[i * length : (i + 1) * length]
        panels.append(lax.all_gather(piece, "col"))
    diag_factor, q_parts = factorize(diag_matrix, row_count, col_count)
    top_parts = solve_top(tops, q_parts, col_count)
    outs = ()
    for i in range(CHUNKS):
        outs = update_rows(panels[i], q_parts, top_parts, trailing, i * length, outs, col_count)
    return (diag_factor, *outs)


def solution(mesh):
    in_specs = (P("row", "col"), P("row", "col"), P("row", "col"))
    out_specs = (P("row", "col"), P("row", "col"), P("row", "col"))
    return jax.shard_map(shards, mesh=mesh, in_specs=in_specs, out_specs=out_specs, check_vma=False)
```

```python
import functools

import jax
import jax.numpy as jnp
from jax import lax
from jax.experimental import pallas as pl
from jax.experimental.pallas import tpu as pltpu
from jax.sharding import PartitionSpec as P

BLOCK = 128
TILE = 8


def full_dot(left, right, dims):
    return lax.dot_general(
        left, right, (dims, ((), ())), precision=lax.Precision.HIGHEST, preferred_element_type=jnp.float32
    )


def one_hot_dot(value, move, pieces):
    total = None
    rest = value
    for _ in range(pieces):
        piece = rest.astype(jnp.bfloat16)
        rest = rest - piece.astype(jnp.float32)
        part = lax.dot_general(move, piece, (((1,), (0,)), ((), ())), preferred_element_type=jnp.float32)
        total = part if total is None else total + part
    return total


def eliminate(s_ref, r_ref, base):
    count = BLOCK // TILE
    shape = (TILE, BLOCK)
    lane = lax.broadcasted_iota(jnp.int32, shape, 1)
    tiles = [s_ref[base + t * TILE : base + (t + 1) * TILE, base : base + BLOCK] for t in range(count)]
    for p in range(count):
        first = p * TILE
        own = tiles[p]
        rows = [jnp.broadcast_to(own[j : j + 1, :], shape) for j in range(TILE)]
        a = [
            [jnp.broadcast_to(rows[i][:, first + j : first + j + 1], shape) for j in range(i + 1)]
            for i in range(TILE)
        ]
        cols = {
            t: [jnp.broadcast_to(tiles[t][:, first + j : first + j + 1], shape) for j in range(TILE)]
            for t in range(p + 1, count)
        }
        for k in range(TILE):
            scale = lax.rsqrt(a[k][k])
            low = [a[i][k] * scale for i in range(k + 1, TILE)]
            row = rows[k] * scale
            r_ref[first + k : first + k + 1, :] = row[0:1, :]
            used = row + jnp.where(lane == first + k, scale, 0.0)
            for i in range(k + 1, TILE):
                rows[i] = rows[i] - low[i - k - 1] * used
                for j in range(k + 1, i + 1):
                    a[i][j] = a[i][j] - low[i - k - 1] * low[j - k - 1]
            for t in range(p + 1, count):
                col = cols[t][k] * scale
                tiles[t] = tiles[t] - col * used
                for j in range(k + 1, TILE):
                    cols[t][j] = cols[t][j] - col * low[j - k - 1]


def split(value):
    high = value.astype(jnp.bfloat16)
    return high, (value - high.astype(jnp.float32)).astype(jnp.bfloat16)


def split_rows(value):
    high, low = split(value)
    return jnp.concatenate([high, high, low], axis=0)


def split_dot(left, right_parts):
    high, low = split(left)
    return lax.dot_general(
        jnp.concatenate([high, low, high], axis=1),
        right_parts,
        (((1,), (0,)), ((), ())),
        preferred_element_type=jnp.float32,
    )


def gather_kernel(row_count, col_count, d_ref, g_ref, own_sem, col_send, col_recv, row_send, row_recv):
    r = lax.axis_index("row")
    c = lax.axis_index("col")
    along_col = [(r, lax.rem(c + d, col_count)) for d in range(1, col_count)]
    along_row = [(lax.rem(r + d, row_count), c) for d in range(1, row_count)]
    barrier = pltpu.get_barrier_semaphore()
    for peer in along_col + along_row:
        pl.semaphore_signal(barrier, inc=1, device_id=peer, device_id_type=pl.DeviceIdType.MESH)
    pl.semaphore_wait(barrier, row_count + col_count - 2)
    copies = [pltpu.make_async_copy(d_ref, g_ref.at[r, c], own_sem)]
    for i, peer in enumerate(along_col):
        copies.append(
            pltpu.make_async_remote_copy(
                src_ref=d_ref, dst_ref=g_ref.at[r, c], send_sem=col_send.at[i], recv_sem=col_recv.at[i],
                device_id=peer, device_id_type=pl.DeviceIdType.MESH,
            )
        )
    for copy in copies:
        copy.start()
    for copy in copies:
        copy.wait()
    copies = [
        pltpu.make_async_remote_copy(
            src_ref=g_ref.at[r], dst_ref=g_ref.at[r], send_sem=row_send.at[i], recv_sem=row_recv.at[i],
            device_id=peer, device_id_type=pl.DeviceIdType.MESH,
        )
        for i, peer in enumerate(along_row)
    ]
    for copy in copies:
        copy.start()
    for copy in copies:
        copy.wait()


def gather_blocks(block, row_count, col_count):
    dma = pltpu.SemaphoreType.DMA
    return pl.pallas_call(
        functools.partial(gather_kernel, row_count, col_count),
        out_shape=jax.ShapeDtypeStruct((row_count, col_count) + block.shape, block.dtype),
        in_specs=[pl.BlockSpec(memory_space=pltpu.VMEM)],
        out_specs=pl.BlockSpec(memory_space=pltpu.VMEM),
        scratch_shapes=[dma, dma((col_count - 1,)), dma((col_count - 1,)), dma((row_count - 1,)), dma((row_count - 1,))],
        compiler_params=pltpu.CompilerParams(collective_id=0, has_side_effects=True),
    )(block)


def chol_kernel(row_count, col_count, a_ref, f_ref, q_ref, s_ref, l_ref, x_ref, r_ref):
    width = s_ref.shape[0]
    col = lax.axis_index("col")
    per = width // col_count
    rows_dev = width // row_count
    for r in range(row_count):
        for z in range(col_count):
            s_ref[r * rows_dev : (r + 1) * rows_dev, z * per : (z + 1) * per] = a_ref[r, z]
    natural = lax.broadcasted_iota(jnp.int32, (width, width), 0)
    store = lax.broadcasted_iota(jnp.int32, (width, width), 1)
    from_rows = jnp.where(natural == (store % rows_dev) * row_count + store // rows_dev, 1.0, 0.0).astype(jnp.bfloat16)
    from_cols = jnp.where(natural == (store % per) * col_count + store // per, 1.0, 0.0)
    to_cols = from_cols.T.astype(jnp.bfloat16)
    x_ref[...] = one_hot_dot(s_ref[...], from_rows, 3)
    s_ref[...] = one_hot_dot(x_ref[...].T, from_cols.astype(jnp.bfloat16), 3)
    l_ref[...] = jnp.zeros_like(l_ref)
    x_ref[...] = jnp.zeros_like(x_ref)
    up = lax.broadcasted_iota(jnp.int32, (BLOCK, BLOCK), 0)
    across = lax.broadcasted_iota(jnp.int32, (BLOCK, BLOCK), 1)
    for base in range(0, width, BLOCK):
        end = base + BLOCK
        eliminate(s_ref, r_ref, base)
        both = r_ref[...]
        l_ref[base:end, base:end] = jnp.where(up >= across, both.T, 0.0)
        inv = jnp.where(up > across, both, 0.0) + jnp.where(up == across, 1.0 / both, 0.0)
        x_ref[base:end, base:end] = inv
        if base:
            x_ref[base:end, :base] = -full_dot(
                inv, full_dot(l_ref[base:end, :base], x_ref[:base, :base], ((1,), (0,))), ((1,), (0,))
            )
        if end < width:
            below = full_dot(s_ref[end:, base:end], inv, ((1,), (1,)))
            l_ref[end:, base:end] = below
            s_ref[end:, end:] = s_ref[end:, end:] - full_dot(below, below, ((1,), (1,)))
    s_ref[...] = one_hot_dot(x_ref[...], to_cols, 2)
    q_ref[...] = split_rows(one_hot_dot(s_ref[...].T, to_cols, 2))
    r = lax.axis_index("row")
    c = col
    i0 = lax.broadcasted_iota(jnp.int32, (rows_dev, width), 0)
    i1 = lax.broadcasted_iota(jnp.int32, (rows_dev, width), 1)
    pick_rows = jnp.where(i1 == i0 * row_count + r, 1.0, 0.0)
    j0 = lax.broadcasted_iota(jnp.int32, (per, width), 0)
    j1 = lax.broadcasted_iota(jnp.int32, (per, width), 1)
    pick_cols = jnp.where(j1 == j0 * col_count + c, 1.0, 0.0)
    f_ref[...] = full_dot(full_dot(pick_rows, l_ref[...], ((1,), (0,))), pick_cols, ((1,), (1,)))


def factorize(blocks, row_count, col_count):
    width = blocks.shape[0] * blocks.shape[2]
    tripled = jax.ShapeDtypeStruct((3 * width, width), jnp.bfloat16)
    return pl.pallas_call(
        functools.partial(chol_kernel, row_count, col_count),
        out_shape=(jax.ShapeDtypeStruct((width // row_count, width // col_count), jnp.float32), tripled),
        scratch_shapes=[pltpu.VMEM((width, width), jnp.float32)] * 3 + [pltpu.VMEM((BLOCK, BLOCK), jnp.float32)],
        compiler_params=pltpu.CompilerParams(vmem_limit_bytes=32 * 1024 * 1024),
    )(blocks)


def top_kernel(col_count, q_ref, *refs):
    o_ref, t_ref, g_ref = refs[-3:]
    groups, length, lanes = g_ref.shape
    r = lax.axis_index("row")
    for d in range(groups):
        g_ref[lax.rem(r + d, groups)] = refs[d][...]
    owners = groups // col_count
    width = q_ref.shape[1]
    for h in range(owners):
        left = jnp.concatenate([g_ref[h * col_count + z] for z in range(col_count)], axis=1)
        solved = split_dot(left, q_ref[...])
        for b in range(width // BLOCK):
            t_ref[b, pl.ds(h, length, stride=owners), :] = solved[:, b * BLOCK : (b + 1) * BLOCK]
    for b in range(width // BLOCK):
        high, low = split(t_ref[b].T)
        at = b * BLOCK
        o_ref[at : at + BLOCK, :] = high
        o_ref[width + at : width + at + BLOCK, :] = high
        o_ref[2 * width + at : 2 * width + at + BLOCK, :] = low


def solve_top(pieces, q_parts, col_count):
    groups = len(pieces)
    length, lanes = pieces[0].shape
    width = q_parts.shape[1]
    columns = groups // col_count * length
    return pl.pallas_call(
        functools.partial(top_kernel, col_count),
        out_shape=jax.ShapeDtypeStruct((3 * width, columns), jnp.bfloat16),
        scratch_shapes=[pltpu.VMEM((width // BLOCK, columns, BLOCK), jnp.float32), pltpu.VMEM((groups, length, lanes), jnp.float32)],
        compiler_params=pltpu.CompilerParams(vmem_limit_bytes=56 * 1024 * 1024),
    )(q_parts, *pieces)


def update_kernel(col_count, p_ref, q_ref, t_ref, c_ref, *refs):
    f_ref, n_ref, s_ref = refs[-3:]
    left = jnp.concatenate([p_ref[z] for z in range(col_count)], axis=1)
    solved = split_dot(left, q_ref[...])
    lanes = f_ref.shape[1]
    for z in range(col_count):
        s_ref[z] = solved[:, z * lanes : (z + 1) * lanes]
    f_ref[...] = s_ref[lax.axis_index("col")]
    n_ref[...] = c_ref[...] - split_dot(solved, t_ref[...])


def update_rows(panel, q_parts, top_parts, trailing, offset, previous, col_count):
    _, length, lanes = panel.shape
    rows, columns = trailing.shape
    tile = 256
    first = offset // tile
    fixed = lambda a: pl.BlockSpec(a.shape, lambda i: (0, 0), pipeline_mode=pl.Buffered(1))
    strip = lambda n: pl.BlockSpec((tile, n), lambda i: (first + i, 0))
    flops = 2 * 3 * length * q_parts.shape[1] * (columns + q_parts.shape[1])
    return pl.pallas_call(
        functools.partial(update_kernel, col_count),
        grid=(length // tile,),
        out_shape=(
            jax.ShapeDtypeStruct((rows, lanes), jnp.float32),
            jax.ShapeDtypeStruct((rows, columns), jnp.float32),
        ),
        in_specs=[
            pl.BlockSpec((col_count, tile, lanes), lambda i: (0, i, 0)),
            fixed(q_parts),
            fixed(top_parts),
            strip(columns),
        ]
        + [pl.BlockSpec(memory_space=pl.ANY)] * len(previous),
        out_specs=(strip(lanes), strip(columns)),
        scratch_shapes=[pltpu.VMEM((col_count, tile, lanes), jnp.float32)],
        input_output_aliases={4 + i: i for i in range(len(previous))},
        cost_estimate=pl.CostEstimate(
            flops=flops, bytes_accessed=length * columns * 8, transcendentals=0
        ),
        compiler_params=pltpu.CompilerParams(vmem_limit_bytes=60 * 1024 * 1024),
    )(panel, q_parts, top_parts, trailing, *previous)


def shards(diag_block, panel_below, trailing):
    row_count = lax.axis_size("row")
    col_count = lax.axis_size("col")
    owners = row_count // col_count
    top_length = trailing.shape[1] // owners
    pairs = [
        ((h * col_count + c) * col_count + z, (h * col_count + z) * col_count + c)
        for h in range(owners)
        for c in range(col_count)
        for z in range(col_count)
    ]
    mine = lax.ppermute(panel_below[:top_length], ("row", "col"), pairs)
    rows = panel_below.shape[0]
    cuts = (0, 2 * rows // 3, rows)
    panels = [lax.all_gather(panel_below[a:b], "col") for a, b in zip(cuts, cuts[1:])]
    blocks = gather_blocks(diag_block, row_count, col_count)
    blocks, mine = lax.optimization_barrier((blocks, mine))
    pieces = [mine]
    for d in range(1, row_count):
        pieces.append(lax.ppermute(mine, "row", [((i + d) % row_count, i) for i in range(row_count)]))
    diag_factor, q_parts = factorize(blocks, row_count, col_count)
    top_parts = solve_top(pieces, q_parts, col_count)
    outs = ()
    for panel, start in zip(panels, cuts):
        outs = update_rows(panel, q_parts, top_parts, trailing, start, outs, col_count)
    return (diag_factor, *outs)


def solution(mesh):
    in_specs = (P("row", "col"), P("row", "col"), P("row", "col"))
    out_specs = (P("row", "col"), P("row", "col"), P("row", "col"))
    return jax.shard_map(shards, mesh=mesh, in_specs=in_specs, out_specs=out_specs, check_vma=False)
```

```python
import functools

import jax
import jax.numpy as jnp
from jax import lax
from jax.experimental import pallas as pl
from jax.experimental.pallas import tpu as pltpu
from jax.sharding import PartitionSpec as P

BLOCK = 128
TILE = 8


def full_dot(left, right, dims):
    return lax.dot_general(
        left, right, (dims, ((), ())), precision=lax.Precision.HIGHEST, preferred_element_type=jnp.float32
    )


def one_hot_dot(value, move, pieces):
    total = None
    rest = value
    for _ in range(pieces):
        piece = rest.astype(jnp.bfloat16)
        rest = rest - piece.astype(jnp.float32)
        part = lax.dot_general(move, piece, (((1,), (0,)), ((), ())), preferred_element_type=jnp.float32)
        total = part if total is None else total + part
    return total


def eliminate(s_ref, r_ref, base):
    count = BLOCK // TILE
    shape = (TILE, BLOCK)
    lane = lax.broadcasted_iota(jnp.int32, shape, 1)
    tiles = [s_ref[base + t * TILE : base + (t + 1) * TILE, base : base + BLOCK] for t in range(count)]
    for p in range(count):
        first = p * TILE
        own = tiles[p]
        rows = [jnp.broadcast_to(own[j : j + 1, :], shape) for j in range(TILE)]
        a = [
            [jnp.broadcast_to(rows[i][:, first + j : first + j + 1], shape) for j in range(i + 1)]
            for i in range(TILE)
        ]
        cols = {
            t: [jnp.broadcast_to(tiles[t][:, first + j : first + j + 1], shape) for j in range(TILE)]
            for t in range(p + 1, count)
        }
        for k in range(TILE):
            scale = lax.rsqrt(a[k][k])
            low = [a[i][k] * scale for i in range(k + 1, TILE)]
            row = rows[k] * scale
            r_ref[first + k : first + k + 1, :] = row[0:1, :]
            used = row + jnp.where(lane == first + k, scale, 0.0)
            for i in range(k + 1, TILE):
                rows[i] = rows[i] - low[i - k - 1] * used
                for j in range(k + 1, i + 1):
                    a[i][j] = a[i][j] - low[i - k - 1] * low[j - k - 1]
            for t in range(p + 1, count):
                col = cols[t][k] * scale
                tiles[t] = tiles[t] - col * used
                for j in range(k + 1, TILE):
                    cols[t][j] = cols[t][j] - col * low[j - k - 1]


def split(value):
    high = value.astype(jnp.bfloat16)
    return high, (value - high.astype(jnp.float32)).astype(jnp.bfloat16)


def split_rows(value):
    high, low = split(value)
    return jnp.concatenate([high, high, low], axis=0)


def split_dot(left, right_parts):
    high, low = split(left)
    return lax.dot_general(
        jnp.concatenate([high, low, high], axis=1),
        right_parts,
        (((1,), (0,)), ((), ())),
        preferred_element_type=jnp.float32,
    )


def gather_kernel(row_count, col_count, d_ref, g_ref, own_sem, col_send, col_recv, row_send, row_recv):
    r = lax.axis_index("row")
    c = lax.axis_index("col")
    along_col = [(r, lax.rem(c + d, col_count)) for d in range(1, col_count)]
    along_row = [(lax.rem(r + d, row_count), c) for d in range(1, row_count)]
    barrier = pltpu.get_barrier_semaphore()
    for peer in along_col + along_row:
        pl.semaphore_signal(barrier, inc=1, device_id=peer, device_id_type=pl.DeviceIdType.MESH)
    pl.semaphore_wait(barrier, row_count + col_count - 2)
    copies = [pltpu.make_async_copy(d_ref, g_ref.at[r, c], own_sem)]
    for i, peer in enumerate(along_col):
        copies.append(
            pltpu.make_async_remote_copy(
                src_ref=d_ref, dst_ref=g_ref.at[r, c], send_sem=col_send.at[i], recv_sem=col_recv.at[i],
                device_id=peer, device_id_type=pl.DeviceIdType.MESH,
            )
        )
    for copy in copies:
        copy.start()
    for copy in copies:
        copy.wait()
    copies = [
        pltpu.make_async_remote_copy(
            src_ref=g_ref.at[r], dst_ref=g_ref.at[r], send_sem=row_send.at[i], recv_sem=row_recv.at[i],
            device_id=peer, device_id_type=pl.DeviceIdType.MESH,
        )
        for i, peer in enumerate(along_row)
    ]
    for copy in copies:
        copy.start()
    for copy in copies:
        copy.wait()


def gather_blocks(block, row_count, col_count):
    dma = pltpu.SemaphoreType.DMA
    return pl.pallas_call(
        functools.partial(gather_kernel, row_count, col_count),
        out_shape=jax.ShapeDtypeStruct((row_count, col_count) + block.shape, block.dtype),
        in_specs=[pl.BlockSpec(memory_space=pltpu.VMEM)],
        out_specs=pl.BlockSpec(memory_space=pltpu.VMEM),
        scratch_shapes=[dma, dma((col_count - 1,)), dma((col_count - 1,)), dma((row_count - 1,)), dma((row_count - 1,))],
        compiler_params=pltpu.CompilerParams(collective_id=0, has_side_effects=True),
    )(block)


def chol_kernel(row_count, col_count, a_ref, f_ref, q_ref, s_ref, l_ref, x_ref, r_ref):
    width = s_ref.shape[0]
    col = lax.axis_index("col")
    per = width // col_count
    rows_dev = width // row_count
    for r in range(row_count):
        for z in range(col_count):
            s_ref[r * rows_dev : (r + 1) * rows_dev, z * per : (z + 1) * per] = a_ref[r, z]
    natural = lax.broadcasted_iota(jnp.int32, (width, width), 0)
    store = lax.broadcasted_iota(jnp.int32, (width, width), 1)
    from_rows = jnp.where(natural == (store % rows_dev) * row_count + store // rows_dev, 1.0, 0.0).astype(jnp.bfloat16)
    from_cols = jnp.where(natural == (store % per) * col_count + store // per, 1.0, 0.0)
    to_cols = from_cols.T.astype(jnp.bfloat16)
    x_ref[...] = one_hot_dot(s_ref[...], from_rows, 3)
    s_ref[...] = one_hot_dot(x_ref[...].T, from_cols.astype(jnp.bfloat16), 3)
    l_ref[...] = jnp.zeros_like(l_ref)
    x_ref[...] = jnp.zeros_like(x_ref)
    up = lax.broadcasted_iota(jnp.int32, (BLOCK, BLOCK), 0)
    across = lax.broadcasted_iota(jnp.int32, (BLOCK, BLOCK), 1)
    for base in range(0, width, BLOCK):
        end = base + BLOCK
        eliminate(s_ref, r_ref, base)
        both = r_ref[...]
        l_ref[base:end, base:end] = jnp.where(up >= across, both.T, 0.0)
        inv = jnp.where(up > across, both, 0.0) + jnp.where(up == across, 1.0 / both, 0.0)
        x_ref[base:end, base:end] = inv
        if base:
            x_ref[base:end, :base] = -full_dot(
                inv, full_dot(l_ref[base:end, :base], x_ref[:base, :base], ((1,), (0,))), ((1,), (0,))
            )
        if end < width:
            below = full_dot(s_ref[end:, base:end], inv, ((1,), (1,)))
            l_ref[end:, base:end] = below
            s_ref[end:, end:] = s_ref[end:, end:] - full_dot(below, below, ((1,), (1,)))
    s_ref[...] = one_hot_dot(x_ref[...], to_cols, 2)
    q_ref[...] = split_rows(one_hot_dot(s_ref[...].T, to_cols, 2))
    r = lax.axis_index("row")
    c = col
    i0 = lax.broadcasted_iota(jnp.int32, (rows_dev, width), 0)
    i1 = lax.broadcasted_iota(jnp.int32, (rows_dev, width), 1)
    pick_rows = jnp.where(i1 == i0 * row_count + r, 1.0, 0.0)
    j0 = lax.broadcasted_iota(jnp.int32, (per, width), 0)
    j1 = lax.broadcasted_iota(jnp.int32, (per, width), 1)
    pick_cols = jnp.where(j1 == j0 * col_count + c, 1.0, 0.0)
    f_ref[...] = full_dot(full_dot(pick_rows, l_ref[...], ((1,), (0,))), pick_cols, ((1,), (1,)))


def factorize(blocks, row_count, col_count):
    width = blocks.shape[0] * blocks.shape[2]
    tripled = jax.ShapeDtypeStruct((3 * width, width), jnp.bfloat16)
    return pl.pallas_call(
        functools.partial(chol_kernel, row_count, col_count),
        out_shape=(jax.ShapeDtypeStruct((width // row_count, width // col_count), jnp.float32), tripled),
        scratch_shapes=[pltpu.VMEM((width, width), jnp.float32)] * 3 + [pltpu.VMEM((BLOCK, BLOCK), jnp.float32)],
        compiler_params=pltpu.CompilerParams(vmem_limit_bytes=32 * 1024 * 1024),
    )(blocks)


def top_kernel(col_count, q_ref, *refs):
    o_ref, t_ref, g_ref = refs[-3:]
    groups, length, lanes = g_ref.shape
    r = lax.axis_index("row")
    for d in range(groups):
        g_ref[lax.rem(r + d, groups)] = refs[d][...]
    owners = groups // col_count
    width = q_ref.shape[1]
    for h in range(owners):
        left = jnp.concatenate([g_ref[h * col_count + z] for z in range(col_count)], axis=1)
        solved = split_dot(left, q_ref[...])
        for b in range(width // BLOCK):
            t_ref[b, pl.ds(h, length, stride=owners), :] = solved[:, b * BLOCK : (b + 1) * BLOCK]
    for b in range(width // BLOCK):
        high, low = split(t_ref[b].T)
        at = b * BLOCK
        o_ref[at : at + BLOCK, :] = high
        o_ref[width + at : width + at + BLOCK, :] = high
        o_ref[2 * width + at : 2 * width + at + BLOCK, :] = low


def solve_top(pieces, q_parts, col_count):
    groups = len(pieces)
    length, lanes = pieces[0].shape
    width = q_parts.shape[1]
    columns = groups // col_count * length
    return pl.pallas_call(
        functools.partial(top_kernel, col_count),
        out_shape=jax.ShapeDtypeStruct((3 * width, columns), jnp.bfloat16),
        scratch_shapes=[pltpu.VMEM((width // BLOCK, columns, BLOCK), jnp.float32), pltpu.VMEM((groups, length, lanes), jnp.float32)],
        compiler_params=pltpu.CompilerParams(vmem_limit_bytes=56 * 1024 * 1024),
    )(q_parts, *pieces)


def update_kernel(col_count, p_ref, q_ref, t_ref, c_ref, *refs):
    f_ref, n_ref, s_ref = refs[-3:]
    left = jnp.concatenate([p_ref[z] for z in range(col_count)], axis=1)
    solved = split_dot(left, q_ref[...])
    lanes = f_ref.shape[1]
    for z in range(col_count):
        s_ref[z] = solved[:, z * lanes : (z + 1) * lanes]
    f_ref[...] = s_ref[lax.axis_index("col")]
    n_ref[...] = c_ref[...] - split_dot(solved, t_ref[...])


def update_rows(panel, q_parts, top_parts, trailing, offset, previous, col_count):
    _, length, lanes = panel.shape
    rows, columns = trailing.shape
    tile = 256
    first = offset // tile
    fixed = lambda a: pl.BlockSpec(a.shape, lambda i: (0, 0), pipeline_mode=pl.Buffered(1))
    strip = lambda n: pl.BlockSpec((tile, n), lambda i: (first + i, 0))
    flops = 2 * 3 * length * q_parts.shape[1] * (columns + q_parts.shape[1])
    return pl.pallas_call(
        functools.partial(update_kernel, col_count),
        grid=(length // tile,),
        out_shape=(
            jax.ShapeDtypeStruct((rows, lanes), jnp.float32),
            jax.ShapeDtypeStruct((rows, columns), jnp.float32),
        ),
        in_specs=[
            pl.BlockSpec((col_count, tile, lanes), lambda i: (0, i, 0)),
            fixed(q_parts),
            fixed(top_parts),
            strip(columns),
        ]
        + [pl.BlockSpec(memory_space=pl.ANY)] * len(previous),
        out_specs=(strip(lanes), strip(columns)),
        scratch_shapes=[pltpu.VMEM((col_count, tile, lanes), jnp.float32)],
        input_output_aliases={4 + i: i for i in range(len(previous))},
        cost_estimate=pl.CostEstimate(
            flops=flops, bytes_accessed=length * columns * 8, transcendentals=0
        ),
        compiler_params=pltpu.CompilerParams(vmem_limit_bytes=60 * 1024 * 1024),
    )(panel, q_parts, top_parts, trailing, *previous)


def shards(diag_block, panel_below, trailing):
    row_count = lax.axis_size("row")
    col_count = lax.axis_size("col")
    owners = row_count // col_count
    top_length = trailing.shape[1] // owners
    pairs = [
        ((h * col_count + c) * col_count + z, (h * col_count + z) * col_count + c)
        for h in range(owners)
        for c in range(col_count)
        for z in range(col_count)
    ]
    mine = lax.ppermute(panel_below[:top_length], ("row", "col"), pairs)
    blocks = gather_blocks(diag_block, row_count, col_count)
    blocks, mine, panel = lax.optimization_barrier((blocks, mine, panel_below))
    rows = panel.shape[0]
    cuts = (0, 5 * rows // 6, rows)
    panels = [lax.all_gather(panel[a:b], "col") for a, b in zip(cuts, cuts[1:])]
    pieces = [mine]
    for d in range(1, row_count):
        pieces.append(lax.ppermute(mine, "row", [((i + d) % row_count, i) for i in range(row_count)]))
    diag_factor, q_parts = factorize(blocks, row_count, col_count)
    top_parts = solve_top(pieces, q_parts, col_count)
    outs = ()
    for panel, start in zip(panels, cuts):
        outs = update_rows(panel, q_parts, top_parts, trailing, start, outs, col_count)
    return (diag_factor, *outs)


def solution(mesh):
    in_specs = (P("row", "col"), P("row", "col"), P("row", "col"))
    out_specs = (P("row", "col"), P("row", "col"), P("row", "col"))
    return jax.shard_map(shards, mesh=mesh, in_specs=in_specs, out_specs=out_specs, check_vma=False)
```
